32 devices in a mesh: group: 4 (over y, core), member: 8 (over z, x).
Axes of the slice: x: 2, y: 2, z: 4, core: 2. Of those that a mesh axis runs over, the one named last changes fastest.
Arguments:
- position: float32 [3, 262144], P(None, ('group', 'member')), may hold values from -6 to 6
- velocity: float32 [3, 262144], P(None, ('group', 'member')), may hold values from -6 to 6
- mass: float32 [262144], P(('group', 'member')), may hold values from 0.0009765625 to 0.0078125
- neighbours: int32 [2048, 4], P(('group', 'member')), may hold values from 0 to 71
- list_length: int32 [2048], P(('group', 'member')), may hold values from 1 to 4
- let_list: int32 [32, 8], P(('group', 'member')), may hold values from 0 to 63
- cell_list: int32 [32, 32], P(('group', 'member')), may hold values from 0 to 511
- destination: int32 [2, 2048], P(None, ('group', 'member')), may hold values from 0 to 7, as said below
Outputs:
- final_position: float32 [3, 262144], P(None, ('group', 'member'))
- final_velocity: float32 [3, 262144], P(None, ('group', 'member'))
- final_mass: float32 [262144], P(('group', 'member'))
The draws below stay inside these ranges and needn't reach their ends.
Inputs may be any that keep to these rules, and one draw needn't show every extreme that they name: `neighbours`: index into the pool of the block's device: its 64 own blocks, then one block from each member of its group in member order. Only the first list_length entries of a block's list are used. `destination`: in each step and group, all devices move the block in slot b the same number of places along member, wrapping around, so every device receives exactly one block for each slot; a device sends at most 8 blocks to one device, and in every step and group some device sends exactly that many to one device.
All inputs are finite; a program needn't handle non-finite values.
Results may differ from the reference program's by a relative error of at most 0.0003.
Values sent between devices are 32-bit elements; how exact they have to be, the bound alone decides.
A program may use at most 64 MiB of HBM per device.

```python
import math
import jax
import jax.numpy as jnp
from jax import lax

BLOCK = 128
NB = 64
CELL = 16
LIST = 4
MSEND = 32
PDEV = 8192
BLOCKS = 2048
TOTAL = 262144
POOL = 72
MCAP = 8
NCELL = 512
N_GROUP = 4
N_MEMBER = 8


def draw_destination(key, part):
    base_key = jax.random.fold_in(key, 11)
    keys_all = jax.random.split(base_key, 2 * N_GROUP)

    def offsets_for(one_key):
        first_key, second_key = jax.random.split(one_key)
        slot_order = jax.random.permutation(first_key, NB)
        chosen_offsets = jax.random.permutation(second_key, N_MEMBER)
        return chosen_offsets[slot_order // MCAP]
    offsets = jax.vmap(offsets_for)(keys_all).reshape(2, N_GROUP, 1, NB)
    members = jnp.arange(N_MEMBER, dtype=jnp.int32).reshape(1, 1, N_MEMBER, 1)
    return ((members + offsets) % N_MEMBER).reshape(2, N_GROUP * N_MEMBER * NB).astype(jnp.int32)


def draw_position(key, part):
    device_count = N_GROUP * N_MEMBER
    side = int(math.ceil(device_count ** (1.0 / 3.0) - 1e-09))
    if side ** 3 < device_count:
        side = side + 1
    columns = jnp.arange(TOTAL, dtype=jnp.int32)
    device = columns // PDEV
    lattice = jnp.stack([device % side, device // side % side, device // (side * side)], axis=0).astype(jnp.float32)
    centre = -3.4 + 6.8 * (lattice + 0.5) / side
    cell_key, point_key = jax.random.split(jax.random.fold_in(key, 23))
    cell_count = TOTAL // CELL
    cell_offset = jnp.clip(0.25 * jax.random.normal(cell_key, (3, cell_count), jnp.float32), -1.0, 1.0)
    point_offset = jnp.clip(0.05 * jax.random.normal(point_key, (3, TOTAL), jnp.float32), -0.2, 0.2)
    cell_spread = jnp.repeat(cell_offset, CELL, axis=1)
    return (centre + cell_spread + point_offset).astype(jnp.float32)


def set_ends(values, stream_key, low, largest):
    longest = values.shape.index(max(values.shape))
    spots = []
    for shift in (0, 1):
        where = [jax.random.randint(jax.random.fold_in(stream_key, axis), (), 0, length) for axis, length in enumerate(values.shape)]
        where[longest] = (where[longest] + shift) % values.shape[longest]
        spots.append(tuple(where))
    return values.at[spots[0]].set(low).at[spots[1]].set(largest)


def block_levels(key, extent, pieces, least, largest):
    level = 1.0
    for dim, parts in pieces:
        steps = jax.random.uniform(jax.random.fold_in(jax.random.fold_in(key, 6), dim), (parts,), jnp.float32, least / len(pieces), largest / len(pieces))
        level = level * jnp.repeat(jnp.exp(steps), extent[dim] // parts).reshape((-1,) + (1,) * (len(extent) - 1 - dim))
    return level


def bell_draw(own_key, shape, width, reach, pieces=(), kind=jnp.bfloat16):
    gain = block_levels(own_key, shape, pieces, -0.22, 0.18) if pieces else 1.0
    drawn = jax.random.normal(own_key, shape, jnp.float32) * width * gain
    return jnp.minimum(jnp.maximum(drawn, -reach), reach).astype(kind)


def setup_inputs(seed: int = 0) -> dict:
    keys = jax.random.split(jax.random.key(seed), 9)
    return {
        "position": draw_position(jax.random.fold_in(keys[8], 71), 0),
        "velocity": bell_draw(keys[1], (3, TOTAL), 1.0, 6.0, ((1, 32),), jnp.float32),
        "mass": jnp.clip(jnp.exp(math.log(0.0078125) - 2.0794415 * jax.random.uniform(keys[2], (TOTAL,), jnp.float32) ** block_levels(keys[2], (TOTAL,), ((0, 32),), -0.2, 0.2)), 0.0009765625, 0.0078125),
        "neighbours": set_ends(jax.random.randint(keys[3], (BLOCKS, LIST), 0, POOL), jax.random.fold_in(keys[3], 1), 0, POOL - 1).astype(jnp.int32),
        "list_length": set_ends(jax.random.randint(keys[4], (BLOCKS,), max(1, LIST // 4), LIST + 1), jax.random.fold_in(keys[4], 1), max(1, LIST // 4), LIST).astype(jnp.int32),
        "let_list": set_ends(jax.random.randint(keys[5], (N_GROUP * N_MEMBER, N_MEMBER), 0, NB), jax.random.fold_in(keys[5], 1), 0, NB - 1).astype(jnp.int32),
        "cell_list": set_ends(jax.random.randint(keys[6], (N_GROUP * N_MEMBER, MSEND), 0, NCELL), jax.random.fold_in(keys[6], 1), 0, NCELL - 1).astype(jnp.int32),
        "destination": draw_destination(jax.random.fold_in(keys[8], 71), 0),
    }


SOFTENING = 0.01
TIMESTEP = 0.1

def pull_toward(targets, sources):
    offset = sources[:3, :, None] - targets[:, None, :]
    radius_sq = lax.optimization_barrier(jnp.sum(offset * offset, axis=0)) + SOFTENING
    inverse = lax.rsqrt(radius_sq)
    weight = sources[3][:, None] * inverse * inverse * inverse
    return lax.optimization_barrier(jnp.sum(offset * weight[None], axis=1))

def all_forces(halfway, mass, neighbours, list_length, let_list, cell_list):
    layout = (N_GROUP, N_MEMBER, NB, BLOCK)
    coords = halfway.reshape((3,) + layout)
    weights = mass.reshape((1,) + layout)
    blocks = jnp.concatenate([coords, weights], axis=0)
    remote_index = let_list.reshape(N_GROUP, N_MEMBER, N_MEMBER)
    sent = jnp.take_along_axis(blocks, remote_index[None, :, :, :, None], axis=3)
    received = jnp.swapaxes(sent, 2, 3)
    source_pool = jnp.concatenate([blocks, received], axis=3)
    cell_mass = weights[0].reshape(N_GROUP, N_MEMBER, NB * BLOCK // CELL, CELL).sum(-1)
    cell_centre = (coords * weights).reshape(3, N_GROUP, N_MEMBER, NB * BLOCK // CELL, CELL).sum(-1) / cell_mass
    cells = jnp.concatenate([cell_centre, cell_mass[None]], axis=0)
    chosen_cells = jnp.take_along_axis(cells, cell_list.reshape(1, N_GROUP, N_MEMBER, MSEND), axis=3)
    lists = neighbours.reshape(N_GROUP, N_MEMBER, NB, LIST)
    lengths = list_length.reshape(N_GROUP, N_MEMBER, NB)

    def per_device(device):
        group_here = device // N_MEMBER
        member_here = device % N_MEMBER
        targets = coords[:, group_here, member_here]
        pool_here = source_pool[:, group_here, member_here]
        far_cells = chosen_cells[:, :, member_here]
        keep_group = (jnp.arange(N_GROUP, dtype=jnp.int32) != group_here).astype(far_cells.dtype)
        far_sources = jnp.concatenate([far_cells[:3], (far_cells[3] * keep_group[:, None])[None]], axis=0).reshape(4, -1)

        def one_block(block_targets, block_list, block_length):
            chosen = pool_here[:, block_list]
            live = (jnp.arange(LIST, dtype=jnp.int32) < block_length).astype(chosen.dtype)
            sources = jnp.concatenate([chosen[:3], (chosen[3] * live[:, None])[None]], axis=0).reshape(4, -1)
            return pull_toward(block_targets, sources) + pull_toward(block_targets, far_sources)
        return jax.vmap(one_block, in_axes=(1, 0, 0), out_axes=1)(targets, lists[group_here, member_here], lengths[group_here, member_here])
    result = lax.map(per_device, jnp.arange(N_GROUP * N_MEMBER, dtype=jnp.int32))
    return jnp.moveaxis(result, 1, 0).reshape(3, -1)

def migrate(position, velocity, mass, target_flat):
    block_state = jnp.concatenate([position, velocity, mass[None]], axis=0).reshape(7, N_GROUP, N_MEMBER, NB, BLOCK)
    target_member = target_flat.reshape(N_GROUP, N_MEMBER, NB)
    group_rows = jnp.arange(N_GROUP, dtype=jnp.int32)[:, None, None]
    slot_rows = jnp.arange(NB, dtype=jnp.int32)[None, None, :]
    moved_state = jnp.zeros_like(block_state).at[:, group_rows, target_member, slot_rows].set(block_state)
    flattened = moved_state.reshape(7, -1)
    return (flattened[0:3], flattened[3:6], flattened[6])

def reference(position, velocity, mass, neighbours, list_length, let_list, cell_list, destination):
    for turn_index in range(2):
        halfway = position + 0.5 * TIMESTEP * velocity
        acceleration = all_forces(halfway, mass, neighbours, list_length, let_list, cell_list)
        velocity = velocity + TIMESTEP * acceleration
        position = halfway + 0.5 * TIMESTEP * velocity
        position, velocity, mass = migrate(position, velocity, mass, destination[turn_index])
    return (position, velocity, mass)
```

```python
import functools

import jax
import jax.numpy as jnp
from jax import lax
from jax.experimental import pallas as pl
from jax.experimental.pallas import tpu as pltpu
from jax.sharding import PartitionSpec as P

BLOCK = 128
CELL = 16
SOFTENING = 0.01
TIMESTEP = 0.1
ROWS = 8
FEATS = 64
HALF = 0.5 * TIMESTEP


def parts_of(value):
    high = value.astype(jnp.bfloat16).astype(jnp.float32)
    rest = value - high
    middle = rest.astype(jnp.bfloat16).astype(jnp.float32)
    return high, middle, rest - middle


def rows_of(shape):
    return lax.broadcasted_iota(jnp.int32, shape, 0)


def source_features(block):
    row = rows_of(block.shape)
    mass = block[3:4]
    square = jnp.sum(jnp.where(row < 3, block * block, 0.0), axis=0, keepdims=True)
    tail = jnp.where(row == 3, square, jnp.where(row == 4, 1.0, 0.0))
    high, middle, low = parts_of(jnp.where(row < 3, block, tail))
    columns = jnp.concatenate([high, high, high, middle, middle, middle, low, low], axis=0)
    weighted = jnp.where(row < 3, block * mass, jnp.where(row == 3, mass, 0.0))
    moments = jnp.concatenate(parts_of(weighted) + (jnp.zeros_like(weighted),), axis=0)
    return jnp.transpose(columns).astype(jnp.bfloat16), moments.astype(jnp.bfloat16)


def target_features(block):
    row = rows_of(block.shape)
    square = jnp.sum(jnp.where(row < 3, block * block, 0.0), axis=0, keepdims=True)
    tail = jnp.where(row == 3, 1.0, jnp.where(row == 4, square + SOFTENING, 0.0))
    high, middle, low = parts_of(jnp.where(row < 3, -2.0 * block, tail))
    rows = jnp.concatenate([high, middle, low, high, middle, low, high, middle], axis=0)
    return rows.astype(jnp.bfloat16)


def moments_of(columns, moments, targets):
    radius_sq = jnp.dot(columns, targets, preferred_element_type=jnp.float32)
    inverse = lax.rsqrt(radius_sq)
    weight = (inverse * inverse * inverse).astype(jnp.bfloat16)
    return jnp.dot(moments, weight, preferred_element_type=jnp.float32)


def fold(sums):
    return sums[0:ROWS] + sums[ROWS : 2 * ROWS] + sums[2 * ROWS : 3 * ROWS]


def kernel(
    sizes,
    ints,
    position,
    velocity,
    mass,
    out_position,
    out_velocity,
    out_mass,
    half,
    speed,
    columns,
    moments,
    targets,
    far,
    far_columns,
    far_moments,
    let_out,
    let_in,
    cell_out,
    cell_in,
    move_out,
    move_in,
    let_send,
    let_recv,
    cell_send,
    cell_recv,
    move_send,
    move_recv,
):
    blocks, entries, members, groups, capacity, publish = sizes
    slots = members * capacity
    chunks = far_columns.shape[0]
    per_chunk = groups // chunks
    lengths_at = blocks * entries
    let_at = lengths_at + blocks
    cells_at = let_at + members
    order_at = cells_at + publish
    slot_at = order_at + 2 * slots
    group, member = lax.axis_index("group"), lax.axis_index("member")

    def peer(distance):
        return {"member": lax.rem(member + distance, members)}

    def group_peer(distance):
        return {"group": lax.rem(group + distance, groups)}

    mesh_id = pl.DeviceIdType.MESH
    barrier = pltpu.get_barrier_semaphore()
    for distance in range(1, members):
        pl.semaphore_signal(barrier, inc=1, device_id=peer(distance), device_id_type=mesh_id)
    for distance in range(1, groups):
        pl.semaphore_signal(barrier, inc=1, device_id=group_peer(distance), device_id_type=mesh_id)

    def let_copy(turn, distance):
        return pltpu.make_async_remote_copy(
            src_ref=let_out.at[turn, distance],
            dst_ref=let_in.at[turn, distance],
            send_sem=let_send.at[turn, distance],
            recv_sem=let_recv.at[turn, distance],
            device_id=peer(distance),
            device_id_type=mesh_id,
        )

    def cell_copy(turn, distance):
        return pltpu.make_async_remote_copy(
            src_ref=cell_out.at[turn],
            dst_ref=cell_in.at[turn, distance],
            send_sem=cell_send.at[turn, distance],
            recv_sem=cell_recv.at[turn, distance],
            device_id=group_peer(distance),
            device_id_type=mesh_id,
        )

    def move_copy(turn, distance):
        return pltpu.make_async_remote_copy(
            src_ref=move_out.at[turn, distance],
            dst_ref=move_in.at[turn, distance],
            send_sem=move_send.at[turn, distance],
            recv_sem=move_recv.at[turn, distance],
            device_id=peer(distance),
            device_id_type=mesh_id,
        )

    def arrived(turn, block):
        slot = ints[slot_at + turn * blocks + block]
        return move_in[turn, slot // capacity, slot % capacity]

    speed[...] = jnp.zeros_like(speed)
    half[...] = jnp.zeros_like(half)
    row = rows_of((ROWS, BLOCK))
    lane = lax.broadcasted_iota(jnp.int32, (ROWS, BLOCK), 1)

    for turn in range(2):

        def load_block(block, _):
            at = pl.ds(pl.multiple_of(block * BLOCK, BLOCK), BLOCK)
            if turn == 0:
                place, pace = position[:, at], velocity[:, at]
                heft = mass[pl.ds(block, 1), :]
            else:
                state = arrived(0, block)
                place, pace, heft = state[0:3], state[4:7], state[3:4]
            half[block, 0:3, :] = place + HALF * pace
            half[block, 3:4, :] = heft
            speed[block, 0:3, :] = pace
            return 0

        lax.fori_loop(0, blocks, load_block, 0, unroll=4)

        for distance in range(members):
            listed = ints[let_at + lax.rem(member + distance, members)]
            whole = half[listed]
            if distance == 0:
                let_in[turn, 0] = whole[0:4]
            else:
                let_out[turn, distance] = whole[0:4]
        if turn == 0:
            pl.semaphore_wait(barrier, members + groups - 2)
        for distance in range(1, members):
            let_copy(turn, distance).start()

        per_block = BLOCK // CELL
        offset = lax.rem(group, per_chunk) * publish
        found = jnp.zeros((ROWS, BLOCK), jnp.float32)
        for entry in range(publish):
            cell = ints[cells_at + entry]
            block = half[cell // per_block]
            heft = block[3:4]
            weighted = jnp.where(row < 3, block * heft, block)
            inside = lane // CELL == cell % per_block
            total = jnp.sum(jnp.where(inside, weighted, 0.0), axis=1, keepdims=True)
            found = jnp.where(lane == offset + entry, total, found)
        held = (lane >= offset) & (lane < offset + publish)
        heft = jnp.where(held, found[3:4], 1.0)
        found = jnp.where(row < 3, found / heft, found)
        if chunks > 1:
            cell_out[turn] = jnp.zeros_like(cell_out[turn])
        cell_out[turn, group // per_chunk] = found
        for distance in range(1, groups):
            cell_copy(turn, distance).start()

        def featurise(block, _):
            here = half[block]
            columns[block], moments[block] = source_features(here)
            targets[block] = target_features(here)
            return 0

        lax.fori_loop(0, blocks, featurise, 0, unroll=4)

        for distance in range(1, groups):
            cell_copy(turn, distance).wait_recv()
        for chunk in range(chunks):
            total = cell_in[turn, 1, chunk]
            for distance in range(2, groups):
                total = total + cell_in[turn, distance, chunk]
            far_columns[chunk], far_moments[chunk] = source_features(total)

        def far_pair(pair, _):
            two = jnp.concatenate([targets[2 * pair], targets[2 * pair + 1]], axis=1)
            total = moments_of(far_columns[0], far_moments[0], two)
            for chunk in range(1, chunks):
                total = total + moments_of(far_columns[chunk], far_moments[chunk], two)
            total = fold(total)
            far[2 * pair], far[2 * pair + 1] = total[:, :BLOCK], total[:, BLOCK:]
            return 0

        lax.fori_loop(0, blocks // 2, far_pair, 0, unroll=2)

        for distance in range(1, members):
            let_copy(turn, distance).wait_recv()

        def featurise_listed(distance, _):
            spread = jnp.concatenate(
                [let_in[turn, distance], jnp.zeros((4, BLOCK), jnp.float32)], axis=0
            )
            columns[blocks + distance], moments[blocks + distance] = source_features(spread)
            return 0

        lax.fori_loop(0, members, featurise_listed, 0, unroll=2)

        width = 4 if capacity % 4 == 0 else capacity

        def near(distance, into):
            def some(step, _):
                results = []
                for inner in range(width):
                    rank = step * width + inner
                    block = ints[order_at + turn * slots + distance * capacity + rank]
                    goal = targets[block]
                    length = ints[lengths_at + block]
                    total = None
                    for entry in range(entries):
                        source = ints[block * entries + entry]
                        live = (entry < length).astype(jnp.float32).astype(jnp.bfloat16)
                        term = moments_of(columns[source], moments[source] * live, goal)
                        total = term if total is None else total + term
                    sums = fold(total) + far[block]
                    here = half[block]
                    pull = jnp.where(row < 3, sums - here * sums[3:4], 0.0)
                    pace = speed[block] + TIMESTEP * pull
                    results.append((rank, here + HALF * pace, pace))
                for rank, place, pace in results:
                    into[turn, distance, rank, 0:4, :] = place[0:4]
                    into[turn, distance, rank, 4:7, :] = pace[0:3]
                return 0

            lax.fori_loop(0, capacity // width, some, 0)

        def send_away(index, _):
            swing = (index + 1) // 2
            distance = members // 2 + jnp.where(index % 2 == 1, -swing, swing)
            near(distance, move_out)
            move_copy(turn, distance).start()
            return 0

        lax.fori_loop(0, members - 1, send_away, 0)
        near(0, move_in)
        for distance in range(1, members):
            move_copy(turn, distance).wait_recv()

    def unload(block, _):
        at = pl.ds(pl.multiple_of(block * BLOCK, BLOCK), BLOCK)
        state = arrived(1, block)
        out_position[:, at] = state[0:3]
        out_velocity[:, at] = state[4:7]
        out_mass[pl.ds(block, 1), :] = state[3:4]
        return 0

    lax.fori_loop(0, blocks, unload, 0, unroll=4)
    for turn in range(2):
        for distance in range(1, members):
            let_copy(turn, distance).wait_send()
            move_copy(turn, distance).wait_send()
        for distance in range(1, groups):
            cell_copy(turn, distance).wait_send()


def shards(position, velocity, mass, neighbours, list_length, let_list, cell_list, destination):
    members, groups = lax.axis_size("member"), lax.axis_size("group")
    member = lax.axis_index("member")
    blocks, entries = neighbours.shape
    publish = cell_list.shape[1]
    capacity = (blocks + members - 1) // members
    slots = members * capacity
    chunks = max(1, groups * publish // BLOCK)

    shift = (destination - member) % members
    number = jnp.arange(blocks, dtype=jnp.int32)
    same = (shift[:, :, None] == shift[:, None, :]) & (number[None, :] < number[:, None])
    slot = shift * capacity + jnp.sum(same, axis=2, dtype=jnp.int32)
    hit = slot[:, None, :] == jnp.arange(slots, dtype=jnp.int32)[None, :, None]
    order = jnp.sum(jnp.where(hit, number[None, None, :], 0), axis=2, dtype=jnp.int32)
    pool = jnp.where(
        neighbours < blocks, neighbours, blocks + (member - (neighbours - blocks)) % members
    )
    ints = jnp.concatenate(
        [
            pool.reshape(-1),
            list_length,
            let_list.reshape(-1),
            cell_list.reshape(-1),
            order.reshape(-1),
            slot.reshape(-1),
        ]
    )
    vmem = pl.BlockSpec(memory_space=pltpu.VMEM)
    f32, bf16 = jnp.float32, jnp.bfloat16
    pool_size = blocks + members
    dma = pltpu.SemaphoreType.DMA
    results = pl.pallas_call(
        functools.partial(kernel, (blocks, entries, members, groups, capacity, publish)),
        out_shape=(
            jax.ShapeDtypeStruct(position.shape, f32),
            jax.ShapeDtypeStruct(velocity.shape, f32),
            jax.ShapeDtypeStruct((blocks, BLOCK), f32),
        ),
        in_specs=[pl.BlockSpec(memory_space=pltpu.SMEM), vmem, vmem, vmem],
        out_specs=(vmem, vmem, vmem),
        scratch_shapes=[
            pltpu.VMEM((blocks, ROWS, BLOCK), f32),
            pltpu.VMEM((blocks, ROWS, BLOCK), f32),
            pltpu.VMEM((pool_size, BLOCK, FEATS), bf16),
            pltpu.VMEM((pool_size, 4 * ROWS, BLOCK), bf16),
            pltpu.VMEM((blocks, FEATS, BLOCK), bf16),
            pltpu.VMEM((blocks, ROWS, BLOCK), f32),
            pltpu.VMEM((chunks, BLOCK, FEATS), bf16),
            pltpu.VMEM((chunks, 4 * ROWS, BLOCK), bf16),
            pltpu.VMEM((2, members, 4, BLOCK), f32),
            pltpu.VMEM((2, members, 4, BLOCK), f32),
            pltpu.VMEM((2, chunks, ROWS, BLOCK), f32),
            pltpu.VMEM((2, groups, chunks, ROWS, BLOCK), f32),
            pltpu.VMEM((2, members, capacity, 7, BLOCK), f32),
            pltpu.VMEM((2, members, capacity, 7, BLOCK), f32),
            dma((2, members)),
            dma((2, members)),
            dma((2, groups)),
            dma((2, groups)),
            dma((2, members)),
            dma((2, members)),
        ],
        compiler_params=pltpu.CompilerParams(
            collective_id=0, has_side_effects=True, vmem_limit_bytes=48 * 1024 * 1024
        ),
        name="two_steps",
    )(ints, position, velocity, mass.reshape(blocks, BLOCK))
    return results[0], results[1], results[2].reshape(-1)


def solution(mesh):
    shared = ("group", "member")
    return jax.shard_map(
        shards,
        mesh=mesh,
        in_specs=(
            P(None, shared),
            P(None, shared),
            P(shared),
            P(shared, None),
            P(shared),
            P(shared, None),
            P(shared, None),
            P(None, shared),
        ),
        out_specs=(P(None, shared), P(None, shared), P(shared)),
        check_vma=False,
    )
```

```python
import functools

import jax
import jax.numpy as jnp
from jax import lax
from jax.experimental import pallas as pl
from jax.experimental.pallas import tpu as pltpu
from jax.sharding import PartitionSpec as P

BLOCK = 128
CELL = 16
SOFTENING = 0.01
TIMESTEP = 0.1
ROWS = 8
FEATS = 64
HALF = 0.5 * TIMESTEP


def parts_of(value):
    high = value.astype(jnp.bfloat16).astype(jnp.float32)
    rest = value - high
    middle = rest.astype(jnp.bfloat16).astype(jnp.float32)
    return high, middle, rest - middle


def rows_of(shape):
    return lax.broadcasted_iota(jnp.int32, shape, 0)


def source_features(block):
    row = rows_of(block.shape)
    mass = block[3:4]
    square = jnp.sum(jnp.where(row < 3, block * block, 0.0), axis=0, keepdims=True)
    tail = jnp.where(row == 3, square, jnp.where(row == 4, 1.0, 0.0))
    high, middle, low = parts_of(jnp.where(row < 3, block, tail))
    columns = jnp.concatenate([high, high, high, middle, middle, middle, low, low], axis=0)
    weighted = jnp.where(row < 3, block * mass, jnp.where(row == 3, mass, 0.0))
    moments = jnp.concatenate(parts_of(weighted) + (jnp.zeros_like(weighted),), axis=0)
    return jnp.transpose(columns).astype(jnp.bfloat16), moments.astype(jnp.bfloat16)


def target_features(block):
    row = rows_of(block.shape)
    square = jnp.sum(jnp.where(row < 3, block * block, 0.0), axis=0, keepdims=True)
    tail = jnp.where(row == 3, 1.0, jnp.where(row == 4, square + SOFTENING, 0.0))
    high, middle, low = parts_of(jnp.where(row < 3, -2.0 * block, tail))
    rows = jnp.concatenate([high, middle, low, high, middle, low, high, middle], axis=0)
    return rows.astype(jnp.bfloat16)


def weighted_sums(radius_sq, moments):
    inverse = lax.rsqrt(radius_sq)
    weight = (inverse * inverse * inverse).astype(jnp.bfloat16)
    return jnp.dot(moments, weight, preferred_element_type=jnp.float32)


def moments_of(columns, moments, targets):
    return weighted_sums(
        jnp.dot(columns, targets, preferred_element_type=jnp.float32), moments
    )


def fold(sums):
    return sums[0:ROWS] + sums[ROWS : 2 * ROWS] + sums[2 * ROWS : 3 * ROWS]


def kernel(
    sizes,
    ints,
    position,
    velocity,
    mass,
    out_position,
    out_velocity,
    out_mass,
    half,
    speed,
    columns,
    moments,
    targets,
    far,
    far_columns,
    far_moments,
    let_out,
    let_in,
    cell_out,
    cell_in,
    move_out,
    move_in,
    let_send,
    let_recv,
    cell_send,
    cell_recv,
    move_send,
    move_recv,
):
    blocks, entries, members, groups, capacity, publish = sizes
    slots = members * capacity
    chunks = far_columns.shape[0]
    per_chunk = groups // chunks
    lengths_at = blocks * entries
    let_at = lengths_at + blocks
    cells_at = let_at + members
    order_at = cells_at + publish
    slot_at = order_at + 2 * slots
    group, member = lax.axis_index("group"), lax.axis_index("member")

    def peer(distance):
        return {"member": lax.rem(member + distance, members)}

    def group_peer(distance):
        return {"group": lax.rem(group + distance, groups)}

    mesh_id = pl.DeviceIdType.MESH
    barrier = pltpu.get_barrier_semaphore()
    for distance in range(1, members):
        pl.semaphore_signal(barrier, inc=1, device_id=peer(distance), device_id_type=mesh_id)
    for distance in range(1, groups):
        pl.semaphore_signal(barrier, inc=1, device_id=group_peer(distance), device_id_type=mesh_id)

    def let_copy(turn, distance):
        return pltpu.make_async_remote_copy(
            src_ref=let_out.at[turn, distance],
            dst_ref=let_in.at[turn, distance],
            send_sem=let_send.at[turn, distance],
            recv_sem=let_recv.at[turn, distance],
            device_id=peer(distance),
            device_id_type=mesh_id,
        )

    def cell_copy(turn, distance):
        return pltpu.make_async_remote_copy(
            src_ref=cell_out.at[turn],
            dst_ref=cell_in.at[turn, distance],
            send_sem=cell_send.at[turn, distance],
            recv_sem=cell_recv.at[turn, distance],
            device_id=group_peer(distance),
            device_id_type=mesh_id,
        )

    def move_copy(turn, distance):
        return pltpu.make_async_remote_copy(
            src_ref=move_out.at[turn, distance],
            dst_ref=move_in.at[turn, distance],
            send_sem=move_send.at[turn, distance],
            recv_sem=move_recv.at[turn, distance],
            device_id=peer(distance),
            device_id_type=mesh_id,
        )

    def arrived(turn, block):
        slot = ints[slot_at + turn * blocks + block]
        return move_in[turn, slot // capacity, slot % capacity]

    speed[...] = jnp.zeros_like(speed)
    half[...] = jnp.zeros_like(half)
    row = rows_of((ROWS, BLOCK))
    lane = lax.broadcasted_iota(jnp.int32, (ROWS, BLOCK), 1)

    for turn in range(2):

        def load_block(block, _):
            at = pl.ds(pl.multiple_of(block * BLOCK, BLOCK), BLOCK)
            if turn == 0:
                place, pace = position[:, at], velocity[:, at]
                heft = mass[pl.ds(block, 1), :]
            else:
                state = arrived(0, block)
                place, pace, heft = state[0:3], state[4:7], state[3:4]
            half[block, 0:3, :] = place + HALF * pace
            half[block, 3:4, :] = heft
            speed[block, 0:3, :] = pace
            return 0

        lax.fori_loop(0, blocks, load_block, 0, unroll=4)

        for distance in range(members):
            listed = ints[let_at + lax.rem(member + distance, members)]
            whole = half[listed]
            if distance == 0:
                let_in[turn, 0] = whole[0:4]
            else:
                let_out[turn, distance] = whole[0:4]
        if turn == 0:
            pl.semaphore_wait(barrier, members + groups - 2)
        for distance in range(1, members):
            let_copy(turn, distance).start()

        per_block = BLOCK // CELL
        offset = lax.rem(group, per_chunk) * publish
        found = jnp.zeros((ROWS, BLOCK), jnp.float32)
        for entry in range(publish):
            cell = ints[cells_at + entry]
            block = half[cell // per_block]
            heft = block[3:4]
            weighted = jnp.where(row < 3, block * heft, block)
            inside = lane // CELL == cell % per_block
            total = jnp.sum(jnp.where(inside, weighted, 0.0), axis=1, keepdims=True)
            found = jnp.where(lane == offset + entry, total, found)
        held = (lane >= offset) & (lane < offset + publish)
        heft = jnp.where(held, found[3:4], 1.0)
        found = jnp.where(row < 3, found / heft, found)
        if chunks > 1:
            cell_out[turn] = jnp.zeros_like(cell_out[turn])
        cell_out[turn, group // per_chunk] = found
        for distance in range(1, groups):
            cell_copy(turn, distance).start()

        def featurise(block, _):
            here = half[block]
            columns[block], moments[block] = source_features(here)
            targets[block] = target_features(here)
            return 0

        lax.fori_loop(0, blocks, featurise, 0, unroll=4)

        for distance in range(1, groups):
            cell_copy(turn, distance).wait_recv()
        for chunk in range(chunks):
            total = cell_in[turn, 1, chunk]
            for distance in range(2, groups):
                total = total + cell_in[turn, distance, chunk]
            far_columns[chunk], far_moments[chunk] = source_features(total)

        wide = 4 if blocks % 8 == 0 else 1

        def far_pairs(step, _):
            pairs = [step * wide + inner for inner in range(wide)]

            def radius_of(pair):
                two = jnp.concatenate([targets[2 * pair], targets[2 * pair + 1]], axis=1)
                return [
                    jnp.dot(far_columns[chunk], two, preferred_element_type=jnp.float32)
                    for chunk in range(chunks)
                ]

            results = []
            ahead = radius_of(pairs[0])
            for inner in range(wide):
                now = ahead
                if inner + 1 < wide:
                    ahead = radius_of(pairs[inner + 1])
                total = weighted_sums(now[0], far_moments[0])
                for chunk in range(1, chunks):
                    total = total + weighted_sums(now[chunk], far_moments[chunk])
                results.append(fold(total))
            for pair, total in zip(pairs, results):
                far[2 * pair], far[2 * pair + 1] = total[:, :BLOCK], total[:, BLOCK:]
            return 0

        lax.fori_loop(0, blocks // (2 * wide), far_pairs, 0)

        for distance in range(1, members):
            let_copy(turn, distance).wait_recv()

        def featurise_listed(distance, _):
            spread = jnp.concatenate(
                [let_in[turn, distance], jnp.zeros((4, BLOCK), jnp.float32)], axis=0
            )
            columns[blocks + distance], moments[blocks + distance] = source_features(spread)
            return 0

        lax.fori_loop(0, members, featurise_listed, 0, unroll=2)

        width = 8 if capacity % 8 == 0 else capacity

        def near(distance, into):
            def some(step, _):
                ranks = [step * width + inner for inner in range(width)]
                at = order_at + turn * slots + distance * capacity
                owned = [ints[at + rank] for rank in ranks]

                def radius_of(block):
                    near_columns = jnp.concatenate(
                        [columns[ints[block * entries + entry]] for entry in range(entries)], axis=0
                    )
                    return jnp.dot(near_columns, targets[block], preferred_element_type=jnp.float32)

                results = []
                ahead = radius_of(owned[0])
                for inner in range(width):
                    block, radius_sq = owned[inner], ahead
                    if inner + 1 < width:
                        ahead = radius_of(owned[inner + 1])
                    length = ints[lengths_at + block]
                    near_moments = jnp.concatenate(
                        [
                            moments[ints[block * entries + entry]]
                            * (entry < length).astype(jnp.float32).astype(jnp.bfloat16)
                            for entry in range(entries)
                        ],
                        axis=1,
                    )
                    sums = fold(weighted_sums(radius_sq, near_moments)) + far[block]
                    here = half[block]
                    pull = jnp.where(row < 3, sums - here * sums[3:4], 0.0)
                    pace = speed[block] + TIMESTEP * pull
                    results.append((ranks[inner], here + HALF * pace, pace))
                for rank, place, pace in results:
                    into[turn, distance, rank, 0:4, :] = place[0:4]
                    into[turn, distance, rank, 4:7, :] = pace[0:3]
                return 0

            lax.fori_loop(0, capacity // width, some, 0)

        def send_away(index, _):
            swing = (index + 1) // 2
            distance = members // 2 + jnp.where(index % 2 == 1, -swing, swing)
            near(distance, move_out)
            move_copy(turn, distance).start()
            return 0

        lax.fori_loop(0, members - 1, send_away, 0)
        near(0, move_in)
        for distance in range(1, members):
            move_copy(turn, distance).wait_recv()

    def unload(block, _):
        at = pl.ds(pl.multiple_of(block * BLOCK, BLOCK), BLOCK)
        state = arrived(1, block)
        out_position[:, at] = state[0:3]
        out_velocity[:, at] = state[4:7]
        out_mass[pl.ds(block, 1), :] = state[3:4]
        return 0

    lax.fori_loop(0, blocks, unload, 0, unroll=4)
    for turn in range(2):
        for distance in range(1, members):
            let_copy(turn, distance).wait_send()
            move_copy(turn, distance).wait_send()
        for distance in range(1, groups):
            cell_copy(turn, distance).wait_send()


def shards(position, velocity, mass, neighbours, list_length, let_list, cell_list, destination):
    members, groups = lax.axis_size("member"), lax.axis_size("group")
    member = lax.axis_index("member")
    blocks, entries = neighbours.shape
    publish = cell_list.shape[1]
    capacity = (blocks + members - 1) // members
    slots = members * capacity
    chunks = max(1, groups * publish // BLOCK)

    shift = (destination - member) % members
    number = jnp.arange(blocks, dtype=jnp.int32)
    same = (shift[:, :, None] == shift[:, None, :]) & (number[None, :] < number[:, None])
    slot = shift * capacity + jnp.sum(same, axis=2, dtype=jnp.int32)
    hit = slot[:, None, :] == jnp.arange(slots, dtype=jnp.int32)[None, :, None]
    order = jnp.sum(jnp.where(hit, number[None, None, :], 0), axis=2, dtype=jnp.int32)
    pool = jnp.where(
        neighbours < blocks, neighbours, blocks + (member - (neighbours - blocks)) % members
    )
    ints = jnp.concatenate(
        [
            pool.reshape(-1),
            list_length,
            let_list.reshape(-1),
            cell_list.reshape(-1),
            order.reshape(-1),
            slot.reshape(-1),
        ]
    )
    vmem = pl.BlockSpec(memory_space=pltpu.VMEM)
    f32, bf16 = jnp.float32, jnp.bfloat16
    pool_size = blocks + members
    dma = pltpu.SemaphoreType.DMA
    results = pl.pallas_call(
        functools.partial(kernel, (blocks, entries, members, groups, capacity, publish)),
        out_shape=(
            jax.ShapeDtypeStruct(position.shape, f32),
            jax.ShapeDtypeStruct(velocity.shape, f32),
            jax.ShapeDtypeStruct((blocks, BLOCK), f32),
        ),
        in_specs=[pl.BlockSpec(memory_space=pltpu.SMEM), vmem, vmem, vmem],
        out_specs=(vmem, vmem, vmem),
        scratch_shapes=[
            pltpu.VMEM((blocks, ROWS, BLOCK), f32),
            pltpu.VMEM((blocks, ROWS, BLOCK), f32),
            pltpu.VMEM((pool_size, BLOCK, FEATS), bf16),
            pltpu.VMEM((pool_size, 4 * ROWS, BLOCK), bf16),
            pltpu.VMEM((blocks, FEATS, BLOCK), bf16),
            pltpu.VMEM((blocks, ROWS, BLOCK), f32),
            pltpu.VMEM((chunks, BLOCK, FEATS), bf16),
            pltpu.VMEM((chunks, 4 * ROWS, BLOCK), bf16),
            pltpu.VMEM((2, members, 4, BLOCK), f32),
            pltpu.VMEM((2, members, 4, BLOCK), f32),
            pltpu.VMEM((2, chunks, ROWS, BLOCK), f32),
            pltpu.VMEM((2, groups, chunks, ROWS, BLOCK), f32),
            pltpu.VMEM((2, members, capacity, 7, BLOCK), f32),
            pltpu.VMEM((2, members, capacity, 7, BLOCK), f32),
            dma((2, members)),
            dma((2, members)),
            dma((2, groups)),
            dma((2, groups)),
            dma((2, members)),
            dma((2, members)),
        ],
        compiler_params=pltpu.CompilerParams(
            collective_id=0, has_side_effects=True, vmem_limit_bytes=48 * 1024 * 1024
        ),
        name="two_steps",
    )(ints, position, velocity, mass.reshape(blocks, BLOCK))
    return results[0], results[1], results[2].reshape(-1)


def solution(mesh):
    shared = ("group", "member")
    return jax.shard_map(
        shards,
        mesh=mesh,
        in_specs=(
            P(None, shared),
            P(None, shared),
            P(shared),
            P(shared, None),
            P(shared),
            P(shared, None),
            P(shared, None),
            P(None, shared),
        ),
        out_specs=(P(None, shared), P(None, shared), P(shared)),
        check_vma=False,
    )
```
